32 devices in a mesh: group: 4 (over x, core), blk: 8 (over z, y).
Axes of the slice: x: 2, y: 2, z: 4, core: 2. Of those that a mesh axis runs over, the one named last changes fastest.
Arguments:
- vertex: float32 [32768, 256], P(('group', 'blk')), may hold values from -1.5 to 1.5
- vertex_state: float32 [32768], P(('group', 'blk')), may hold values from 0.1 to 1
- context: float32 [16384, 256], P(('group', 'blk')), may hold values from -1.5 to 1.5
- context_state: float32 [16384], P(('group', 'blk')), may hold values from 0.1 to 1
- tile_weights: bfloat16 [4, 8, 4, 6, 3, 128, 128], P('group', 'blk'), may hold values from 0.049804688 to 2
- tile_rows: int32 [4, 8, 4, 6, 3], P('group', 'blk'), may hold values from 0 to 7
- tile_cols: int32 [4, 8, 4, 6, 3], P('group', 'blk'), may hold values from 0 to 3
- tile_counts: int32 [4, 8, 4, 6], P('group', 'blk'), may hold values from 1 to 3, as said below
- negatives: int32 [4, 8, 6, 8, 2], P('group', 'blk'), may hold values from 0 to 3
Outputs:
- vertex_out: float32 [32768, 256], P(('group', 'blk'))
- vertex_state_out: float32 [32768], P(('group', 'blk'))
- context_out: float32 [16384, 256], P(('group', 'blk'))
- context_state_out: float32 [16384], P(('group', 'blk'))
The draws below stay inside these ranges and needn't reach their ends.
Inputs may be any that keep to these rules, and one draw needn't show every extreme that they name: `tile_counts`: at each stop and each index of blk some destination of the group receives 3 used slots from every walk owner.
All inputs are finite; a program needn't handle non-finite values.
Results may differ from the reference program's by a relative error of at most 0.0049.
Values may be sent and summed in bfloat16 or wider, within the bound.
A program may use at most 64 MiB of HBM per device.

```python
import math
import jax
import jax.numpy as jnp
from jax import lax

D = 256
TILE = 128
CTX = 512
R_DEV = 1024
STEPS = 6
CAP = 3
NNEG = 2
RT = 8
CT = 4
NV = 32768
NC = 16384
N_GROUP = 4
N_BLK = 8


def draw_tile_counts(key, part):
    first = jax.random.fold_in(key, 71)
    second = jax.random.fold_in(key, 72)
    base = jax.random.randint(first, (N_GROUP, N_BLK, N_GROUP, STEPS), 1, CAP + 1)
    chosen = jax.random.randint(second, (1, N_BLK, 1, STEPS), 0, N_GROUP)
    target = jnp.arange(N_GROUP)[None, None, :, None]
    return jnp.where(target == chosen, CAP, base).astype(jnp.int32)


def touch_ends(array, stream_key, smallest, top_value):
    spot = [jax.random.randint(jax.random.fold_in(stream_key, axis), (), 0, length) for axis, length in enumerate(array.shape)]
    longest = array.shape.index(max(array.shape))
    next_to = spot[:longest] + [(spot[longest] + 1) % array.shape[longest]] + spot[longest + 1:]
    return array.at[tuple(spot)].set(smallest).at[tuple(next_to)].set(top_value)


def block_scale(rng, dims, pieces, low, largest):
    gain = 1.0
    for position, blocks in pieces:
        heights = jax.random.uniform(jax.random.fold_in(jax.random.fold_in(rng, 6), position), (blocks,), jnp.float32, low / len(pieces), largest / len(pieces))
        gain = gain * jnp.repeat(jnp.exp(heights), dims[position] // blocks).reshape((-1,) + (1,) * (len(dims) - 1 - position))
    return gain


def gaussian(rng, shape, spread, bound, pieces=(), kind=jnp.bfloat16):
    entries = spread * jax.random.normal(rng, shape, jnp.float32)
    if pieces:
        entries = entries * block_scale(rng, shape, pieces, -0.22, 0.18)
    return jnp.clip(entries, -bound, bound).astype(kind)


def setup_inputs(seed: int = 0) -> dict:
    key_of = jax.random.split(jax.random.key(seed), 10)
    return {
        "vertex": gaussian(key_of[0], (NV, D), 0.25, 1.5, ((0, 32),), jnp.float32),
        "vertex_state": jnp.clip(jnp.exp(math.log(1.0) - 2.3025851 * jax.random.uniform(key_of[1], (NV,), jnp.float32) ** block_scale(key_of[1], (NV,), ((0, 32),), -0.2, 0.2)), 0.1, 1.0),
        "context": gaussian(key_of[2], (NC, D), 0.25, 1.5, ((0, 32),), jnp.float32),
        "context_state": jnp.clip(jnp.exp(math.log(1.0) - 2.3025851 * jax.random.uniform(key_of[3], (NC,), jnp.float32) ** block_scale(key_of[3], (NC,), ((0, 32),), -0.2, 0.2)), 0.1, 1.0),
        "tile_weights": jnp.clip(jnp.exp(math.log(2.0) - 3.6927934 * jax.random.uniform(key_of[4], (N_GROUP, N_BLK, N_GROUP, STEPS, CAP, TILE, TILE), jnp.float32) ** block_scale(key_of[4], (N_GROUP, N_BLK, N_GROUP, STEPS, CAP, TILE, TILE), ((0, 4), (1, 8)), -0.2, 0.2)), 0.049804688, 2.0).astype(jnp.bfloat16),
        "tile_rows": touch_ends(jax.random.randint(key_of[5], (N_GROUP, N_BLK, N_GROUP, STEPS, CAP), 0, RT), jax.random.fold_in(key_of[5], 1), 0, RT - 1).astype(jnp.int32),
        "tile_cols": touch_ends(jax.random.randint(key_of[6], (N_GROUP, N_BLK, N_GROUP, STEPS, CAP), 0, CT), jax.random.fold_in(key_of[6], 1), 0, CT - 1).astype(jnp.int32),
        "tile_counts": draw_tile_counts(jax.random.fold_in(key_of[9], 71), 0),
        "negatives": touch_ends(jax.random.randint(key_of[8], (N_GROUP, N_BLK, STEPS, RT, NNEG), 0, CT), jax.random.fold_in(key_of[8], 1), 0, CT - 1).astype(jnp.int32),
    }


LEARNING = 0.1
NEG_WEIGHT = 0.5

def lowered(values):
    return lax.optimization_barrier(values.astype(jnp.bfloat16)).astype(jnp.float32)

def device_gradients(vertex_rows, context_rows, weights, row_ids, col_ids, negative_ids):
    width = vertex_rows.shape[1]
    tile = weights.shape[-1]
    vertex_tiles = vertex_rows.astype(jnp.bfloat16).astype(jnp.float32).reshape(-1, tile, width)
    context_tiles = context_rows.astype(jnp.bfloat16).astype(jnp.float32).reshape(-1, tile, width)
    vertex_pick = jnp.take(vertex_tiles, row_ids, axis=0)
    context_pick = jnp.take(context_tiles, col_ids, axis=0)
    logits = jnp.einsum('nid,njd->nij', vertex_pick, context_pick)
    pos_grad = lowered(weights.astype(jnp.float32) * (jax.nn.sigmoid(logits) - 1.0))
    vertex_terms = jnp.einsum('nij,njd->nid', pos_grad, context_pick)
    context_terms = jnp.einsum('nij,nid->njd', pos_grad, vertex_pick)
    row_hot = (row_ids[:, None] == jnp.arange(vertex_tiles.shape[0])[None, :]).astype(jnp.float32)
    col_hot = (col_ids[:, None] == jnp.arange(context_tiles.shape[0])[None, :]).astype(jnp.float32)
    vertex_grad = jnp.einsum('nr,nid->rid', row_hot, vertex_terms)
    context_grad = jnp.einsum('nc,njd->cjd', col_hot, context_terms)
    neg_pick = jnp.take(context_tiles, negative_ids, axis=0)
    neg_logits = jnp.einsum('rid,rkjd->rkij', vertex_tiles, neg_pick)
    neg_grad = lowered(NEG_WEIGHT * jax.nn.sigmoid(neg_logits))
    vertex_grad = vertex_grad + jnp.einsum('rkij,rkjd->rid', neg_grad, neg_pick)
    neg_terms = jnp.einsum('rkij,rid->rkjd', neg_grad, vertex_tiles)
    neg_hot = (negative_ids[:, :, None] == jnp.arange(context_tiles.shape[0])[None, None, :]).astype(jnp.float32)
    context_grad = context_grad + jnp.einsum('rkc,rkjd->cjd', neg_hot, neg_terms)
    return (vertex_grad.reshape(-1, width), context_grad.reshape(-1, width))

def adagrad(rows, state, grad):
    new_state = state + lax.optimization_barrier(jnp.mean(grad * grad, axis=1))
    return (rows - LEARNING * grad / jnp.sqrt(new_state)[:, None], new_state)

def reference(vertex, vertex_state, context, context_state, tile_weights, tile_rows, tile_cols, tile_counts, negatives):
    groups = N_GROUP
    blocks = N_BLK
    devices = groups * blocks
    vertex_all = vertex.reshape(devices, R_DEV, D)
    vstate_all = vertex_state.reshape(devices, R_DEV)
    context_all = context.reshape(devices, CTX, D)
    cstate_all = context_state.reshape(devices, CTX)
    received = jnp.transpose(tile_weights, (2, 1, 0, 3, 4, 5, 6))
    rows_all = jnp.transpose(tile_rows, (2, 1, 0, 3, 4)).reshape(devices, groups, STEPS, CAP)
    cols_all = jnp.transpose(tile_cols, (2, 1, 0, 3, 4)).reshape(devices, groups, STEPS, CAP)
    counts_all = jnp.transpose(tile_counts, (2, 1, 0, 3))
    valid = jnp.arange(CAP)[None, None, None, None, :] < counts_all[..., None]
    masked = jnp.where(valid[..., None, None], received, jnp.zeros((), jnp.bfloat16))
    masked = masked.reshape(devices, groups, STEPS, CAP, TILE, TILE)
    neg_all = negatives.reshape(devices, STEPS, RT, NNEG)
    for stop_index in range(STEPS):

        def one_device(items):
            vrows, vstate, crows, cstate, weights, row_ids, col_ids, neg_ids = items
            vertex_grad, context_grad = device_gradients(vrows, crows, weights.reshape(-1, TILE, TILE), row_ids.reshape(-1), col_ids.reshape(-1), neg_ids)
            vrows, vstate = adagrad(vrows, vstate, vertex_grad)
            crows, cstate = adagrad(crows, cstate, context_grad)
            return (vrows, vstate, crows, cstate)
        vertex_all, vstate_all, context_all, cstate_all = lax.map(one_device, (vertex_all, vstate_all, context_all, cstate_all, masked[:, :, stop_index], rows_all[:, :, stop_index], cols_all[:, :, stop_index], neg_all[:, stop_index]))
        if stop_index < STEPS - 1:
            context_all = jnp.roll(context_all.reshape(groups, blocks, CTX, D), 1, axis=1).reshape(devices, CTX, D)
            cstate_all = jnp.roll(cstate_all.reshape(groups, blocks, CTX), 1, axis=1).reshape(devices, CTX)
    return (vertex_all.reshape(-1, D), vstate_all.reshape(-1), context_all.reshape(-1, D), cstate_all.reshape(-1))
```

```python
import functools

import jax
import jax.numpy as jnp
from jax import lax
from jax.experimental import pallas as pl
from jax.experimental.pallas import tpu as pltpu
from jax.sharding import PartitionSpec as P

LEARNING = 0.1
NEG_WEIGHT = 0.5
MESH = pl.DeviceIdType.MESH
SUB = 16


def eye_mask(tile):
    return lax.broadcasted_iota(jnp.int32, (tile, tile), 0) == lax.broadcasted_iota(
        jnp.int32, (tile, tile), 1
    )


def to_column(row):
    tile = row.shape[1]
    return jnp.sum(jnp.where(eye_mask(tile), row, 0.0), axis=1, keepdims=True)


def to_row(column):
    tile = column.shape[0]
    return jnp.sum(jnp.where(eye_mask(tile), column, 0.0), axis=0, keepdims=True)


def kernel(
    sizes,
    vertex_ref,
    vstate_ref,
    context_ref,
    cstate_ref,
    codes_ref,
    negs_ref,
    weights_hbm,
    vout,
    vsout,
    cout,
    csout,
    vb,
    vcol,
    held,
    outgo,
    held_state,
    out_state,
    c32,
    gbuf,
    wagg,
    wbuf,
    codebuf,
    code16,
    hop_send,
    hop_recv,
    st_send,
    st_recv,
    w_send,
    w_recv,
    code_send,
    code_recv,
    own_sem,
    own_code_sem,
):
    n_group, n_blk, steps, cap, row_tiles, ctx_tiles, tile = sizes
    group = lax.axis_index("group")
    blk = lax.axis_index("blk")
    right = lax.rem(blk + 1, n_blk)
    left = lax.rem(blk + n_blk - 1, n_blk)

    def peer(j):
        return lax.rem(group + j, n_group)

    def code_copy(j):
        return pltpu.make_async_remote_copy(
            src_ref=codes_ref.at[peer(j)],
            dst_ref=codebuf.at[j],
            send_sem=code_send.at[j],
            recv_sem=code_recv.at[j],
            device_id={"group": peer(j)},
            device_id_type=MESH,
        )

    def weight_copy(stop, j):
        return pltpu.make_async_remote_copy(
            src_ref=weights_hbm.at[peer(j), stop],
            dst_ref=wbuf.at[stop, j],
            send_sem=w_send.at[stop, j],
            recv_sem=w_recv.at[stop, j],
            device_id={"group": peer(j)},
            device_id_type=MESH,
        )

    def own_copy(stop):
        return pltpu.make_async_copy(
            weights_hbm.at[group, stop], wbuf.at[stop, 0], own_sem.at[stop]
        )

    def own_code():
        return pltpu.make_async_copy(codes_ref.at[group], codebuf.at[0], own_code_sem)

    def hop_copy(stop, c):
        return pltpu.make_async_remote_copy(
            src_ref=outgo.at[stop, c],
            dst_ref=held.at[stop, c],
            send_sem=hop_send.at[stop, c],
            recv_sem=hop_recv.at[stop, c],
            device_id={"blk": right},
            device_id_type=MESH,
        )

    def state_copy(stop, c):
        return pltpu.make_async_remote_copy(
            src_ref=out_state.at[stop, c],
            dst_ref=held_state.at[stop, c],
            send_sem=st_send.at[stop, c],
            recv_sem=st_recv.at[stop, c],
            device_id={"blk": right},
            device_id_type=MESH,
        )

    barrier = pltpu.get_barrier_semaphore()
    pl.semaphore_signal(barrier, inc=1, device_id={"blk": left}, device_id_type=MESH)
    for j in range(1, n_group):
        pl.semaphore_signal(
            barrier, inc=1, device_id={"group": peer(j)}, device_id_type=MESH
        )
    own_code().start()
    for stop in range(steps):
        own_copy(stop).start()
    pl.semaphore_wait(barrier, n_group)

    for j in range(1, n_group):
        code_copy(j).start()
    for stop in range(steps):
        for j in range(1, n_group):
            weight_copy(stop, j).start()

    for r in range(row_tiles):
        rows = slice(r * tile, (r + 1) * tile)
        vb[rows, :] = vertex_ref[rows, :].astype(jnp.bfloat16)
        vout[rows, :] = vertex_ref[rows, :]
        vcol[rows, :] = to_column(vstate_ref[r : r + 1, :])
    for c in range(ctx_tiles):
        held[0, c] = context_ref[c].astype(jnp.bfloat16)
        c32[c] = context_ref[c]
        held_state[0, c] = cstate_ref[c]

    own_code().wait()
    for j in range(1, n_group):
        code_copy(j).wait_recv()
    for j in range(n_group):

        def spread(k, _, j=j):
            code16[j, k] = jnp.broadcast_to(codebuf[j, k], (SUB, tile)).astype(jnp.bfloat16)
            return 0

        lax.fori_loop(0, steps * cap, spread, 0)

    pairs = row_tiles * ctx_tiles
    half = tile // SUB

    def one_stop(s, _):
        own_copy(s).wait()
        for j in range(1, n_group):
            weight_copy(s, j).wait_recv()

        def one_pair(p, _):
            acc = jnp.zeros((half, SUB, tile), jnp.bfloat16)
            here = p.astype(jnp.float32).astype(jnp.bfloat16)
            for j in range(n_group):
                for k in range(cap):
                    hit = jnp.where(
                        code16[j, s * cap + k].astype(jnp.float32) == p.astype(jnp.float32),
                        1.0,
                        0.0,
                    ).astype(jnp.bfloat16)
                    acc = acc + wbuf[s, j, k] * hit[None]
            wagg[p] = acc.reshape(tile, tile)
            return 0

        lax.fori_loop(0, pairs, one_pair, 0)

        for c in range(ctx_tiles):

            @pl.when(s > 0)
            def _():
                hop_copy(s, c).wait_recv()
                state_copy(s, c).wait_recv()
                c32[c] = held[s, c].astype(jnp.float32)

            ctx = held[s, c]
            grad = jnp.zeros(ctx.shape, jnp.float32)
            for r in range(row_tiles):
                rows = slice(r * tile, (r + 1) * tile)
                logits = lax.dot_general(
                    vb[rows, :],
                    ctx,
                    (((1,), (1,)), ((), ())),
                    preferred_element_type=jnp.float32,
                )
                weight = wagg[c * row_tiles + r].astype(jnp.float32)
                scale = 0.5 * (weight + negs_ref[s, c * row_tiles + r])
                g = scale * (1.0 + jnp.tanh(0.5 * logits)) - weight
                g = g.astype(jnp.bfloat16)
                gbuf[rows, c * tile : (c + 1) * tile] = g
            cols = slice(c * tile, (c + 1) * tile)
            grad = lax.dot_general(
                gbuf[:, cols],
                vb[...],
                (((0,), (0,)), ((), ())),
                preferred_element_type=jnp.float32,
            )
            state = to_column(held_state[s, c])
            state = state + jnp.mean(grad * grad, axis=1, keepdims=True)
            new = c32[c] - (LEARNING * grad) * lax.rsqrt(state)
            state_row = to_row(state)

            @pl.when(s < steps - 1)
            def _():
                outgo[s + 1, c] = new.astype(jnp.bfloat16)
                out_state[s + 1, c] = state_row
                hop_copy(s + 1, c).start()
                state_copy(s + 1, c).start()

            @pl.when(s == steps - 1)
            def _():
                cout[c] = new
                csout[c] = state_row

        block = held[s].reshape(ctx_tiles * tile, -1)
        for r in range(row_tiles):
            rows = slice(r * tile, (r + 1) * tile)
            grad = jnp.dot(gbuf[rows, :], block, preferred_element_type=jnp.float32)
            state = vcol[rows, :] + jnp.mean(grad * grad, axis=1, keepdims=True)
            new = vout[rows, :] - (LEARNING * grad) * lax.rsqrt(state)
            vcol[rows, :] = state
            vout[rows, :] = new
            vb[rows, :] = new.astype(jnp.bfloat16)
        return 0

    lax.fori_loop(0, steps, one_stop, 0)

    for r in range(row_tiles):
        vsout[r : r + 1, :] = to_row(vcol[r * tile : (r + 1) * tile, :])

    for j in range(1, n_group):
        code_copy(j).wait_send()
    for stop in range(steps):
        for j in range(1, n_group):
            weight_copy(stop, j).wait_send()
    for stop in range(1, steps):
        for c in range(ctx_tiles):
            hop_copy(stop, c).wait_send()
            state_copy(stop, c).wait_send()


def body(
    n_group,
    n_blk,
    vertex,
    vertex_state,
    context,
    context_state,
    tile_weights,
    tile_rows,
    tile_cols,
    tile_counts,
    negatives,
):
    steps, cap, tile = tile_weights.shape[3], tile_weights.shape[4], tile_weights.shape[5]
    width = vertex.shape[1]
    row_tiles, ctx_tiles = vertex.shape[0] // tile, context.shape[0] // tile
    nneg = negatives.shape[-1]
    half = tile // SUB
    used = jnp.arange(cap)[None, None, :] < tile_counts[0, 0][..., None]
    codes = jnp.where(used, tile_cols[0, 0] * row_tiles + tile_rows[0, 0], -1)
    codes = jnp.broadcast_to(
        codes.reshape(n_group, steps * cap, 1, 1), (n_group, steps * cap, 1, tile)
    ).astype(jnp.float32)
    hits = negatives[0, 0][:, None, :, :] == jnp.arange(ctx_tiles)[None, :, None, None]
    negs = NEG_WEIGHT * jnp.sum(hits.astype(jnp.float32), axis=-1)
    negs = negs.reshape(steps, ctx_tiles * row_tiles)
    sizes = (n_group, n_blk, steps, cap, row_tiles, ctx_tiles, tile)
    vmem = pl.BlockSpec(memory_space=pltpu.VMEM)
    f32, bf16 = jnp.float32, jnp.bfloat16
    dma = pltpu.SemaphoreType.DMA
    vout, vsout, cout, csout = pl.pallas_call(
        functools.partial(kernel, sizes),
        out_shape=(
            jax.ShapeDtypeStruct((row_tiles * tile, width), f32),
            jax.ShapeDtypeStruct((row_tiles, tile), f32),
            jax.ShapeDtypeStruct((ctx_tiles, tile, width), f32),
            jax.ShapeDtypeStruct((ctx_tiles, 1, tile), f32),
        ),
        in_specs=[vmem] * 5
        + [pl.BlockSpec(memory_space=pltpu.SMEM), pl.BlockSpec(memory_space=pl.ANY)],
        out_specs=(vmem,) * 4,
        scratch_shapes=[
            pltpu.VMEM((row_tiles * tile, width), bf16),
            pltpu.VMEM((row_tiles * tile, 1), f32),
            pltpu.VMEM((steps, ctx_tiles, tile, width), bf16),
            pltpu.VMEM((steps, ctx_tiles, tile, width), bf16),
            pltpu.VMEM((steps, ctx_tiles, 1, tile), f32),
            pltpu.VMEM((steps, ctx_tiles, 1, tile), f32),
            pltpu.VMEM((ctx_tiles, tile, width), f32),
            pltpu.VMEM((row_tiles * tile, ctx_tiles * tile), bf16),
            pltpu.VMEM((row_tiles * ctx_tiles, tile, tile), bf16),
            pltpu.VMEM((steps, n_group, cap, half, SUB, tile), bf16),
            pltpu.VMEM((n_group, steps * cap, 1, tile), f32),
            pltpu.VMEM((n_group, steps * cap, SUB, tile), bf16),
            dma((steps, ctx_tiles)),
            dma((steps, ctx_tiles)),
            dma((steps, ctx_tiles)),
            dma((steps, ctx_tiles)),
            dma((steps, n_group)),
            dma((steps, n_group)),
            dma((n_group,)),
            dma((n_group,)),
            dma((steps,)),
            dma,
        ],
        compiler_params=pltpu.CompilerParams(
            collective_id=0, has_side_effects=True, vmem_limit_bytes=48 * 1024 * 1024
        ),
    )(
        vertex,
        vertex_state.reshape(row_tiles, tile),
        context.reshape(ctx_tiles, tile, width),
        context_state.reshape(ctx_tiles, 1, tile),
        codes,
        negs,
        tile_weights.reshape(n_group, steps, cap, half, SUB, tile),
    )
    return (
        vout,
        vsout.reshape(-1),
        cout.reshape(ctx_tiles * tile, width),
        csout.reshape(-1),
    )


def solution(mesh):
    in_specs = (
        P(("group", "blk"), None),
        P(("group", "blk")),
        P(("group", "blk"), None),
        P(("group", "blk")),
        P("group", "blk", None, None, None, None, None),
        P("group", "blk", None, None, None),
        P("group", "blk", None, None, None),
        P("group", "blk", None, None),
        P("group", "blk", None, None, None),
    )
    out_specs = (
        P(("group", "blk"), None),
        P(("group", "blk")),
        P(("group", "blk"), None),
        P(("group", "blk")),
    )
    step = functools.partial(body, mesh.shape["group"], mesh.shape["blk"])
    return jax.shard_map(step, mesh=mesh, in_specs=in_specs, out_specs=out_specs, check_vma=False)
```

```python
import functools

import jax
import jax.numpy as jnp
from jax import lax
from jax.experimental import pallas as pl
from jax.experimental.pallas import tpu as pltpu
from jax.sharding import PartitionSpec as P

LEARNING = 0.1
NEG_WEIGHT = 0.5
MESH = pl.DeviceIdType.MESH
VMEM_LIMIT = 54000000


def eye_mask(tile):
    return lax.broadcasted_iota(jnp.int32, (tile, tile), 0) == lax.broadcasted_iota(
        jnp.int32, (tile, tile), 1
    )


def to_column(row):
    tile = row.shape[1]
    return jnp.sum(jnp.where(eye_mask(tile), row, 0.0), axis=1, keepdims=True)


def to_row(column):
    tile = column.shape[0]
    return jnp.sum(jnp.where(eye_mask(tile), column, 0.0), axis=0, keepdims=True)


def kernel(
    sizes,
    codes_ref,
    negs_ref,
    vertex_hbm,
    vstate_hbm,
    context_hbm,
    cstate_hbm,
    weights_hbm,
    vout,
    vsout,
    cout,
    csout,
    vb,
    vcol,
    held,
    outgo,
    held_state,
    out_state,
    c32,
    gbuf,
    prefix,
    stage,
    wbuf,
    codebuf,
    plan_vmem,
    plan,
    hop_send,
    hop_recv,
    st_send,
    st_recv,
    w_send,
    w_recv,
    code_send,
    code_recv,
    own_sem,
    own_code_sem,
    in_sem,
    plan_sem,
):
    n_group, n_blk, steps, cap, row_tiles, ctx_tiles, tile = sizes
    slots = n_group * cap
    group = lax.axis_index("group")
    blk = lax.axis_index("blk")
    right = lax.rem(blk + 1, n_blk)
    left = lax.rem(blk + n_blk - 1, n_blk)

    def peer(j):
        return lax.rem(group + j, n_group)

    def code_copy(j):
        return pltpu.make_async_remote_copy(
            src_ref=codes_ref.at[:, peer(j)],
            dst_ref=codebuf.at[j],
            send_sem=code_send.at[j],
            recv_sem=code_recv.at[j],
            device_id={"group": peer(j)},
            device_id_type=MESH,
        )

    def weight_copy(stop, j):
        return pltpu.make_async_remote_copy(
            src_ref=weights_hbm.at[peer(j), stop],
            dst_ref=wbuf.at[pl.ds(stop * slots + j * cap, cap)],
            send_sem=w_send.at[stop, j],
            recv_sem=w_recv.at[stop, j],
            device_id={"group": peer(j)},
            device_id_type=MESH,
        )

    def own_copy(stop):
        return pltpu.make_async_copy(
            weights_hbm.at[group, stop],
            wbuf.at[pl.ds(stop * slots, cap)],
            own_sem.at[stop],
        )

    def own_code():
        return pltpu.make_async_copy(codes_ref.at[:, group], codebuf.at[0], own_code_sem)

    def hop_copy(stop, c):
        return pltpu.make_async_remote_copy(
            src_ref=outgo.at[stop, c],
            dst_ref=held.at[stop, c],
            send_sem=hop_send.at[stop, c],
            recv_sem=hop_recv.at[stop, c],
            device_id={"blk": right},
            device_id_type=MESH,
        )

    def state_copy(stop, c):
        return pltpu.make_async_remote_copy(
            src_ref=out_state.at[stop, c],
            dst_ref=held_state.at[stop, c],
            send_sem=st_send.at[stop, c],
            recv_sem=st_recv.at[stop, c],
            device_id={"blk": right},
            device_id_type=MESH,
        )

    barrier = pltpu.get_barrier_semaphore()
    pl.semaphore_signal(barrier, inc=1, device_id={"blk": left}, device_id_type=MESH)
    for j in range(1, n_group):
        pl.semaphore_signal(
            barrier, inc=1, device_id={"group": peer(j)}, device_id_type=MESH
        )
    vertex_in = pltpu.make_async_copy(vertex_hbm, vout, in_sem.at[0])
    context_in = pltpu.make_async_copy(context_hbm, c32, in_sem.at[1])
    vstate_in = pltpu.make_async_copy(vstate_hbm, vsout, in_sem.at[2])
    cstate_in = pltpu.make_async_copy(cstate_hbm, held_state.at[0], in_sem.at[3])
    vstate_in.start()
    cstate_in.start()
    context_in.start()
    vertex_in.start()
    own_code().start()
    for stop in range(steps):
        own_copy(stop).start()
    pl.semaphore_wait(barrier, n_group)

    for j in range(1, n_group):
        code_copy(j).start()
    for stop in range(steps):
        for j in range(1, n_group):
            weight_copy(stop, j).start()

    vstate_in.wait()
    cstate_in.wait()
    context_in.wait()
    vertex_in.wait()
    for r in range(row_tiles):
        rows = slice(r * tile, (r + 1) * tile)
        vb[rows, :] = vout[rows, :].astype(jnp.bfloat16)
        vcol[rows, :] = to_column(vsout[r : r + 1, :])
    for c in range(ctx_tiles):
        held[0, c] = c32[c].astype(jnp.bfloat16)

    own_code().wait()
    for j in range(1, n_group):
        code_copy(j).wait_recv()
    codes = [codebuf[j, k] for j in range(n_group) for k in range(cap)]
    lane = lax.broadcasted_iota(jnp.int32, codes[0].shape, 1)
    upto = jnp.zeros_like(lane)
    below = jnp.zeros_like(lane)
    order = jnp.zeros_like(lane)
    for n, code in enumerate(codes):
        upto = upto + jnp.where(code <= lane, 1, 0)
        below = below + jnp.where(code < lane, 1, 0)
        rank = jnp.zeros_like(lane)
        for m, other in enumerate(codes):
            if m < n:
                rank = rank + jnp.where(other <= code, 1, 0)
            elif m > n:
                rank = rank + jnp.where(other < code, 1, 0)
        order = order + jnp.where(rank == lane, n, 0)
    plan_vmem[0] = upto
    plan_vmem[1] = below
    plan_vmem[2] = order
    plan_copy = pltpu.make_async_copy(plan_vmem, plan, plan_sem)
    plan_copy.start()
    prefix[0] = jnp.zeros((tile, tile), jnp.float32)
    plan_copy.wait()

    def one_stop(s, _):
        own_copy(s).wait()
        for j in range(1, n_group):
            weight_copy(s, j).wait_recv()

        for n in range(slots):
            stage[n] = wbuf[s * slots + n]
        total = jnp.zeros((tile, tile), jnp.float32)
        for n in range(slots):
            total = total + stage[plan[2, s, n]].astype(jnp.float32)
            prefix[n + 1] = total

        for c in range(ctx_tiles):

            @pl.when(s > 0)
            def _():
                hop_copy(s, c).wait_recv()
                state_copy(s, c).wait_recv()
                c32[c] = held[s, c].astype(jnp.float32)

            ctx = held[s, c]
            cols = slice(c * tile, (c + 1) * tile)
            for r in range(row_tiles):
                rows = slice(r * tile, (r + 1) * tile)
                logits = lax.dot_general(
                    vb[rows, :],
                    ctx,
                    (((1,), (1,)), ((), ())),
                    preferred_element_type=jnp.float32,
                )
                pair = c * row_tiles + r
                negative = jnp.float32(0.0)
                for n in range(negs_ref.shape[1]):
                    negative = negative + jnp.where(negs_ref[s, n, r] == c, NEG_WEIGHT, 0.0)
                weight = prefix[plan[0, s, pair]] - prefix[plan[1, s, pair]]
                scale = 0.5 * weight + 0.5 * negative
                g = scale * jnp.tanh(0.5 * logits) + (scale - weight)
                gbuf[rows, cols] = g.astype(jnp.bfloat16)
            grad = lax.dot_general(
                gbuf[:, cols],
                vb[...],
                (((0,), (0,)), ((), ())),
                preferred_element_type=jnp.float32,
            )
            state = to_column(held_state[s, c])
            state = state + jnp.mean(grad * grad, axis=1, keepdims=True)
            new = c32[c] - grad * (LEARNING * lax.rsqrt(state))
            state_row = to_row(state)

            @pl.when(s < steps - 1)
            def _():
                outgo[s + 1, c] = new.astype(jnp.bfloat16)
                out_state[s + 1, c] = state_row
                hop_copy(s + 1, c).start()
                state_copy(s + 1, c).start()

            @pl.when(s == steps - 1)
            def _():
                cout[c] = new
                csout[c] = state_row

        block = held[s].reshape(ctx_tiles * tile, -1)
        for r in range(row_tiles):
            rows = slice(r * tile, (r + 1) * tile)
            grad = jnp.dot(gbuf[rows, :], block, preferred_element_type=jnp.float32)
            state = vcol[rows, :] + jnp.mean(grad * grad, axis=1, keepdims=True)
            new = vout[rows, :] - grad * (LEARNING * lax.rsqrt(state))
            vcol[rows, :] = state
            vout[rows, :] = new
            vb[rows, :] = new.astype(jnp.bfloat16)
        return 0

    lax.fori_loop(0, steps, one_stop, 0)

    for r in range(row_tiles):
        vsout[r : r + 1, :] = to_row(vcol[r * tile : (r + 1) * tile, :])

    for j in range(1, n_group):
        code_copy(j).wait_send()
    for stop in range(steps):
        for j in range(1, n_group):
            weight_copy(stop, j).wait_send()
    for stop in range(1, steps):
        for c in range(ctx_tiles):
            hop_copy(stop, c).wait_send()
            state_copy(stop, c).wait_send()


def put_out(*refs):
    count = len(refs) // 2
    sems = refs[-1]
    copies = [
        pltpu.make_async_copy(refs[i], refs[count + i], sems.at[i]) for i in range(count)
    ]
    for copy in copies:
        copy.start()
    for copy in copies:
        copy.wait()


def body(
    n_group,
    n_blk,
    vertex,
    vertex_state,
    context,
    context_state,
    tile_weights,
    tile_rows,
    tile_cols,
    tile_counts,
    negatives,
):
    steps, cap, tile = tile_weights.shape[3], tile_weights.shape[4], tile_weights.shape[5]
    width = vertex.shape[1]
    row_tiles, ctx_tiles = vertex.shape[0] // tile, context.shape[0] // tile
    pairs = row_tiles * ctx_tiles
    slots = n_group * cap
    assert pairs < tile and slots < tile

    def spread(ids):
        return jnp.broadcast_to(
            ids.transpose(2, 0, 1)[..., None], (cap, n_group, steps, tile)
        )

    used = (
        lax.broadcasted_iota(jnp.int32, (cap, n_group, steps, tile), 0)
        < tile_counts[0, 0][None, :, :, None]
    )
    codes = jnp.where(
        used, spread(tile_cols[0, 0]) * row_tiles + spread(tile_rows[0, 0]), pairs
    )
    sizes = (n_group, n_blk, steps, cap, row_tiles, ctx_tiles, tile)
    vmem = pl.BlockSpec(memory_space=pltpu.VMEM)
    hbm = pl.BlockSpec(memory_space=pltpu.HBM)
    f32, bf16 = jnp.float32, jnp.bfloat16
    dma = pltpu.SemaphoreType.DMA
    outs = (
        jax.ShapeDtypeStruct((row_tiles * tile, width), f32),
        jax.ShapeDtypeStruct((row_tiles, tile), f32),
        jax.ShapeDtypeStruct((ctx_tiles, tile, width), f32),
        jax.ShapeDtypeStruct((ctx_tiles, 1, tile), f32),
    )
    results = pl.pallas_call(
        functools.partial(kernel, sizes),
        out_shape=outs,
        in_specs=[vmem, pl.BlockSpec(memory_space=pltpu.SMEM)] + [hbm] * 5,
        out_specs=(vmem,) * 4,
        scratch_shapes=[
            pltpu.VMEM((row_tiles * tile, width), bf16),
            pltpu.VMEM((row_tiles * tile, 1), f32),
            pltpu.VMEM((steps, ctx_tiles, tile, width), bf16),
            pltpu.VMEM((steps, ctx_tiles, tile, width), bf16),
            pltpu.VMEM((steps, ctx_tiles, 1, tile), f32),
            pltpu.VMEM((steps, ctx_tiles, 1, tile), f32),
            pltpu.VMEM((ctx_tiles, tile, width), f32),
            pltpu.VMEM((row_tiles * tile, ctx_tiles * tile), bf16),
            pltpu.VMEM((slots + 1, tile, tile), f32),
            pltpu.VMEM((slots, tile, tile), bf16),
            pltpu.VMEM((steps * slots, tile, tile), bf16),
            pltpu.VMEM((n_group, cap, steps, tile), jnp.int32),
            pltpu.VMEM((3, steps, tile), jnp.int32),
            pltpu.SMEM((3, steps, tile), jnp.int32),
            dma((steps, ctx_tiles)),
            dma((steps, ctx_tiles)),
            dma((steps, ctx_tiles)),
            dma((steps, ctx_tiles)),
            dma((steps, n_group)),
            dma((steps, n_group)),
            dma((n_group,)),
            dma((n_group,)),
            dma((steps,)),
            dma,
            dma((4,)),
            dma,
        ],
        compiler_params=pltpu.CompilerParams(
            collective_id=0, has_side_effects=True, vmem_limit_bytes=VMEM_LIMIT
        ),
    )(
        codes,
        negatives[0, 0].transpose(0, 2, 1),
        vertex,
        vertex_state.reshape(row_tiles, tile),
        context.reshape(ctx_tiles, tile, width),
        context_state.reshape(ctx_tiles, 1, tile),
        tile_weights.reshape(n_group, steps, cap, tile, tile),
    )
    vout, vsout, cout, csout = pl.pallas_call(
        put_out,
        out_shape=outs,
        in_specs=[vmem] * 4,
        out_specs=(hbm,) * 4,
        scratch_shapes=[dma((4,))],
        compiler_params=pltpu.CompilerParams(vmem_limit_bytes=1024 * 1024),
    )(*results)
    return (
        vout,
        vsout.reshape(-1),
        cout.reshape(ctx_tiles * tile, width),
        csout.reshape(-1),
    )


def solution(mesh):
    in_specs = (
        P(("group", "blk"), None),
        P(("group", "blk")),
        P(("group", "blk"), None),
        P(("group", "blk")),
        P("group", "blk", None, None, None, None, None),
        P("group", "blk", None, None, None),
        P("group", "blk", None, None, None),
        P("group", "blk", None, None),
        P("group", "blk", None, None, None),
    )
    out_specs = (
        P(("group", "blk"), None),
        P(("group", "blk")),
        P(("group", "blk"), None),
        P(("group", "blk")),
    )
    step = functools.partial(body, mesh.shape["group"], mesh.shape["blk"])
    return jax.shard_map(step, mesh=mesh, in_specs=in_specs, out_specs=out_specs, check_vma=False)
```

```python
import functools

import jax
import jax.numpy as jnp
from jax import lax
from jax.experimental import pallas as pl
from jax.experimental.pallas import tpu as pltpu
from jax.sharding import PartitionSpec as P

LEARNING = 0.1
NEG_WEIGHT = 0.5
MESH = pl.DeviceIdType.MESH
VMEM_LIMIT = 54000000


def eye_mask(tile):
    return lax.broadcasted_iota(jnp.int32, (tile, tile), 0) == lax.broadcasted_iota(
        jnp.int32, (tile, tile), 1
    )


def to_column(row):
    tile = row.shape[1]
    return jnp.sum(jnp.where(eye_mask(tile), row, 0.0), axis=1, keepdims=True)


def to_row(column):
    tile = column.shape[0]
    return jnp.sum(jnp.where(eye_mask(tile), column, 0.0), axis=0, keepdims=True)


def kernel(
    sizes,
    codes_ref,
    negs_ref,
    vertex_hbm,
    vstate_hbm,
    context_hbm,
    cstate_hbm,
    weights_hbm,
    vout,
    vsout,
    cout,
    csout,
    vb,
    vcol,
    held,
    outgo,
    held_state,
    out_state,
    c32,
    gbuf,
    prefix,
    stage,
    wbuf,
    codebuf,
    plan_vmem,
    plan,
    hop_send,
    hop_recv,
    st_send,
    st_recv,
    w_send,
    w_recv,
    code_send,
    code_recv,
    own_sem,
    own_code_sem,
    in_sem,
    plan_sem,
):
    n_group, n_blk, steps, cap, row_tiles, ctx_tiles, tile = sizes
    slots = n_group * cap
    group = lax.axis_index("group")
    blk = lax.axis_index("blk")
    right = lax.rem(blk + 1, n_blk)
    left = lax.rem(blk + n_blk - 1, n_blk)

    def peer(j):
        return lax.rem(group + j, n_group)

    def code_copy(j):
        return pltpu.make_async_remote_copy(
            src_ref=codes_ref.at[:, peer(j)],
            dst_ref=codebuf.at[j],
            send_sem=code_send.at[j],
            recv_sem=code_recv.at[j],
            device_id={"group": peer(j)},
            device_id_type=MESH,
        )

    def weight_copy(stop, j):
        return pltpu.make_async_remote_copy(
            src_ref=weights_hbm.at[peer(j), stop],
            dst_ref=wbuf.at[pl.ds(stop * slots + j * cap, cap)],
            send_sem=w_send.at[stop, j],
            recv_sem=w_recv.at[stop, j],
            device_id={"group": peer(j)},
            device_id_type=MESH,
        )

    def own_copy(stop):
        return pltpu.make_async_copy(
            weights_hbm.at[group, stop],
            wbuf.at[pl.ds(stop * slots, cap)],
            own_sem.at[stop],
        )

    def own_code():
        return pltpu.make_async_copy(codes_ref.at[:, group], codebuf.at[0], own_code_sem)

    def hop_copy(stop, c):
        return pltpu.make_async_remote_copy(
            src_ref=outgo.at[stop, c],
            dst_ref=held.at[stop, c],
            send_sem=hop_send.at[stop, c],
            recv_sem=hop_recv.at[stop, c],
            device_id={"blk": right},
            device_id_type=MESH,
        )

    def state_copy(stop, c):
        return pltpu.make_async_remote_copy(
            src_ref=out_state.at[stop, c],
            dst_ref=held_state.at[stop, c],
            send_sem=st_send.at[stop, c],
            recv_sem=st_recv.at[stop, c],
            device_id={"blk": right},
            device_id_type=MESH,
        )

    barrier = pltpu.get_barrier_semaphore()
    pl.semaphore_signal(barrier, inc=1, device_id={"blk": left}, device_id_type=MESH)
    for j in range(1, n_group):
        pl.semaphore_signal(
            barrier, inc=1, device_id={"group": peer(j)}, device_id_type=MESH
        )
    vertex_in = pltpu.make_async_copy(vertex_hbm, vout, in_sem.at[0])
    context_in = pltpu.make_async_copy(context_hbm, c32, in_sem.at[1])
    vstate_in = pltpu.make_async_copy(vstate_hbm, vsout, in_sem.at[2])
    cstate_in = pltpu.make_async_copy(cstate_hbm, held_state.at[0], in_sem.at[3])
    vstate_in.start()
    cstate_in.start()
    context_in.start()
    vertex_in.start()
    own_code().start()
    for stop in range(steps):
        own_copy(stop).start()
    pl.semaphore_wait(barrier, n_group)

    for j in range(1, n_group):
        code_copy(j).start()
    for stop in range(steps):
        for j in range(1, n_group):
            weight_copy(stop, j).start()

    vstate_in.wait()
    cstate_in.wait()
    context_in.wait()
    vertex_in.wait()
    for r in range(row_tiles):
        rows = slice(r * tile, (r + 1) * tile)
        vb[rows, :] = vout[rows, :].astype(jnp.bfloat16)
        vcol[rows, :] = jnp.broadcast_to(to_column(vsout[r : r + 1, :]), (tile, tile))
    for c in range(ctx_tiles):
        held[0, c] = c32[c].astype(jnp.bfloat16)

    own_code().wait()
    for j in range(1, n_group):
        code_copy(j).wait_recv()
    codes = [codebuf[j, k] for j in range(n_group) for k in range(cap)]
    lane = lax.broadcasted_iota(jnp.int32, codes[0].shape, 1)
    upto = jnp.zeros_like(lane)
    below = jnp.zeros_like(lane)
    order = jnp.zeros_like(lane)
    for n, code in enumerate(codes):
        upto = upto + jnp.where(code <= lane, 1, 0)
        below = below + jnp.where(code < lane, 1, 0)
        rank = jnp.zeros_like(lane)
        for m, other in enumerate(codes):
            if m < n:
                rank = rank + jnp.where(other <= code, 1, 0)
            elif m > n:
                rank = rank + jnp.where(other < code, 1, 0)
        order = order + jnp.where(rank == lane, n, 0)
    plan_vmem[0] = upto
    plan_vmem[1] = below
    plan_vmem[2] = order
    plan_copy = pltpu.make_async_copy(plan_vmem, plan, plan_sem)
    plan_copy.start()
    prefix[0] = jnp.zeros((tile, tile), jnp.float32)
    plan_copy.wait()

    width = vb.shape[1]
    batch = 2 if ctx_tiles % 2 == 0 else 1
    spread_mean = jnp.full((width, tile), 1.0 / width, jnp.bfloat16)

    def wide(value):
        return jnp.concatenate([value] * (width // tile), axis=1)

    def mean_square(grad):
        return jnp.dot(
            (grad * grad).astype(jnp.bfloat16), spread_mean, preferred_element_type=jnp.float32
        )

    def one_stop(s, first, last):
        own_copy(s).wait()
        for j in range(1, n_group):
            weight_copy(s, j).wait_recv()

        for n in range(slots):
            stage[n] = wbuf[s * slots + n]
        total = jnp.zeros((tile, tile), jnp.float32)
        for n in range(slots):
            total = total + 0.5 * stage[plan[2, s, n]].astype(jnp.float32)
            prefix[n + 1] = total

        def pair_gradients(first_tile):
            tiles = range(first_tile, first_tile + batch)
            if not first:
                for c in tiles:
                    hop_copy(s, c).wait_recv()
                    state_copy(s, c).wait_recv()
            ctx = held[s, first_tile : first_tile + batch].reshape(batch * tile, width)
            half_logits = lax.dot_general(
                vb[...],
                ctx * jnp.bfloat16(0.5),
                (((1,), (1,)), ((), ())),
                preferred_element_type=jnp.float32,
            )
            for r in range(row_tiles):
                rows = slice(r * tile, (r + 1) * tile)
                for i, c in enumerate(tiles):
                    pair = c * row_tiles + r
                    negative = jnp.float32(0.0)
                    for n in range(negs_ref.shape[1]):
                        negative = negative + jnp.where(
                            negs_ref[s, n, r] == c, 0.5 * NEG_WEIGHT, 0.0
                        )
                    weight = prefix[plan[0, s, pair]] - prefix[plan[1, s, pair]]
                    part = half_logits[rows, i * tile : (i + 1) * tile]
                    g = (negative + weight) * jnp.tanh(part) + (negative - weight)
                    gbuf[rows, c * tile : (c + 1) * tile] = g.astype(jnp.bfloat16)

        def context_update(first_tile):
            grads = lax.dot_general(
                gbuf[:, first_tile * tile : (first_tile + batch) * tile],
                vb[...],
                (((0,), (0,)), ((), ())),
                preferred_element_type=jnp.float32,
            )
            means = mean_square(grads)
            for i in range(batch):
                c = first_tile + i
                part = slice(i * tile, (i + 1) * tile)
                before = jnp.broadcast_to(to_column(held_state[s, c]), (tile, tile))
                state = before + means[part]
                old = c32[c] if first else held[s, c].astype(jnp.float32)
                new = old - grads[part] * wide(LEARNING * lax.rsqrt(state))
                state_row = to_row(state)
                if last:
                    cout[c] = new
                    csout[c] = state_row
                else:
                    outgo[s + 1, c] = new.astype(jnp.bfloat16)
                    out_state[s + 1, c] = state_row
                    hop_copy(s + 1, c).start()
                    state_copy(s + 1, c).start()

        for c in range(0, ctx_tiles, batch):
            pair_gradients(c)
            context_update(c)

        block = held[s].reshape(ctx_tiles * tile, width)
        half = row_tiles // 2
        for h in range(2):
            span = slice(h * half * tile, (h + 1) * half * tile)
            grads = jnp.dot(gbuf[span, :], block, preferred_element_type=jnp.float32)
            state = vcol[span, :] + mean_square(grads)
            new = vout[span, :] - grads * wide(LEARNING * lax.rsqrt(state))
            vcol[span, :] = state
            vout[span, :] = new
            vb[span, :] = new.astype(jnp.bfloat16)

    def middle_stop(s, _):
        one_stop(s, False, False)
        return 0

    one_stop(0, True, steps == 1)
    if steps > 2:
        lax.fori_loop(1, steps - 1, middle_stop, 0)
    if steps > 1:
        one_stop(steps - 1, False, True)

    for r in range(row_tiles):
        vsout[r : r + 1, :] = to_row(vcol[r * tile : (r + 1) * tile, :])

    for j in range(1, n_group):
        code_copy(j).wait_send()
    for stop in range(steps):
        for j in range(1, n_group):
            weight_copy(stop, j).wait_send()
    for stop in range(1, steps):
        for c in range(ctx_tiles):
            hop_copy(stop, c).wait_send()
            state_copy(stop, c).wait_send()


def put_out(*refs):
    count = len(refs) // 2
    sems = refs[-1]
    copies = [
        pltpu.make_async_copy(refs[i], refs[count + i], sems.at[i]) for i in range(count)
    ]
    for copy in copies:
        copy.start()
    for copy in copies:
        copy.wait()


def body(
    n_group,
    n_blk,
    vertex,
    vertex_state,
    context,
    context_state,
    tile_weights,
    tile_rows,
    tile_cols,
    tile_counts,
    negatives,
):
    steps, cap, tile = tile_weights.shape[3], tile_weights.shape[4], tile_weights.shape[5]
    width = vertex.shape[1]
    row_tiles, ctx_tiles = vertex.shape[0] // tile, context.shape[0] // tile
    pairs = row_tiles * ctx_tiles
    slots = n_group * cap
    assert pairs < tile and slots < tile

    def spread(ids):
        return jnp.broadcast_to(
            ids.transpose(2, 0, 1)[..., None], (cap, n_group, steps, tile)
        )

    used = (
        lax.broadcasted_iota(jnp.int32, (cap, n_group, steps, tile), 0)
        < tile_counts[0, 0][None, :, :, None]
    )
    codes = jnp.where(
        used, spread(tile_cols[0, 0]) * row_tiles + spread(tile_rows[0, 0]), pairs
    )
    sizes = (n_group, n_blk, steps, cap, row_tiles, ctx_tiles, tile)
    vmem = pl.BlockSpec(memory_space=pltpu.VMEM)
    hbm = pl.BlockSpec(memory_space=pltpu.HBM)
    f32, bf16 = jnp.float32, jnp.bfloat16
    dma = pltpu.SemaphoreType.DMA
    outs = (
        jax.ShapeDtypeStruct((row_tiles * tile, width), f32),
        jax.ShapeDtypeStruct((row_tiles, tile), f32),
        jax.ShapeDtypeStruct((ctx_tiles, tile, width), f32),
        jax.ShapeDtypeStruct((ctx_tiles, 1, tile), f32),
    )
    results = pl.pallas_call(
        functools.partial(kernel, sizes),
        out_shape=outs,
        in_specs=[vmem, pl.BlockSpec(memory_space=pltpu.SMEM)] + [hbm] * 5,
        out_specs=(vmem,) * 4,
        scratch_shapes=[
            pltpu.VMEM((row_tiles * tile, width), bf16),
            pltpu.VMEM((row_tiles * tile, tile), f32),
            pltpu.VMEM((steps, ctx_tiles, tile, width), bf16),
            pltpu.VMEM((steps, ctx_tiles, tile, width), bf16),
            pltpu.VMEM((steps, ctx_tiles, 1, tile), f32),
            pltpu.VMEM((steps, ctx_tiles, 1, tile), f32),
            pltpu.VMEM((ctx_tiles, tile, width), f32),
            pltpu.VMEM((row_tiles * tile, ctx_tiles * tile), bf16),
            pltpu.VMEM((slots + 1, tile, tile), f32),
            pltpu.VMEM((slots, tile, tile), bf16),
            pltpu.VMEM((steps * slots, tile, tile), bf16),
            pltpu.VMEM((n_group, cap, steps, tile), jnp.int32),
            pltpu.VMEM((3, steps, tile), jnp.int32),
            pltpu.SMEM((3, steps, tile), jnp.int32),
            dma((steps, ctx_tiles)),
            dma((steps, ctx_tiles)),
            dma((steps, ctx_tiles)),
            dma((steps, ctx_tiles)),
            dma((steps, n_group)),
            dma((steps, n_group)),
            dma((n_group,)),
            dma((n_group,)),
            dma((steps,)),
            dma,
            dma((4,)),
            dma,
        ],
        compiler_params=pltpu.CompilerParams(
            collective_id=0, has_side_effects=True, vmem_limit_bytes=VMEM_LIMIT
        ),
    )(
        codes,
        negatives[0, 0].transpose(0, 2, 1),
        vertex,
        vertex_state.reshape(row_tiles, tile),
        context.reshape(ctx_tiles, tile, width),
        context_state.reshape(ctx_tiles, 1, tile),
        tile_weights.reshape(n_group, steps, cap, tile, tile),
    )
    vout, vsout, cout, csout = pl.pallas_call(
        put_out,
        out_shape=outs,
        in_specs=[vmem] * 4,
        out_specs=(hbm,) * 4,
        scratch_shapes=[dma((4,))],
        compiler_params=pltpu.CompilerParams(vmem_limit_bytes=1024 * 1024),
    )(*results)
    return (
        vout,
        vsout.reshape(-1),
        cout.reshape(ctx_tiles * tile, width),
        csout.reshape(-1),
    )


def solution(mesh):
    in_specs = (
        P(("group", "blk"), None),
        P(("group", "blk")),
        P(("group", "blk"), None),
        P(("group", "blk")),
        P("group", "blk", None, None, None, None, None),
        P("group", "blk", None, None, None),
        P("group", "blk", None, None, None),
        P("group", "blk", None, None),
        P("group", "blk", None, None, None),
    )
    out_specs = (
        P(("group", "blk"), None),
        P(("group", "blk")),
        P(("group", "blk"), None),
        P(("group", "blk")),
    )
    step = functools.partial(body, mesh.shape["group"], mesh.shape["blk"])
    return jax.shard_map(step, mesh=mesh, in_specs=in_specs, out_specs=out_specs, check_vma=False)
```

```python
import functools

import jax
import jax.numpy as jnp
from jax import lax
from jax.experimental import pallas as pl
from jax.experimental.pallas import tpu as pltpu
from jax.sharding import PartitionSpec as P

LEARNING = 0.1
NEG_WEIGHT = 0.5
MESH = pl.DeviceIdType.MESH
VMEM_LIMIT = 54000000


def eye_mask(tile):
    return lax.broadcasted_iota(jnp.int32, (tile, tile), 0) == lax.broadcasted_iota(
        jnp.int32, (tile, tile), 1
    )


def to_column(row):
    tile = row.shape[1]
    return jnp.sum(jnp.where(eye_mask(tile), row, 0.0), axis=1, keepdims=True)


def to_row(column):
    tile = column.shape[0]
    return jnp.sum(jnp.where(eye_mask(tile), column, 0.0), axis=0, keepdims=True)


def kernel(
    sizes,
    codes_ref,
    negs_ref,
    vertex_hbm,
    vstate_hbm,
    context_hbm,
    cstate_hbm,
    weights_hbm,
    vout,
    vsout,
    cout,
    csout,
    vb,
    vcol,
    held,
    outgo,
    held_state,
    out_state,
    c32,
    gbuf,
    prefix,
    stage,
    wbuf,
    codebuf,
    plan_vmem,
    plan,
    hop_send,
    hop_recv,
    st_send,
    st_recv,
    w_send,
    w_recv,
    code_send,
    code_recv,
    own_sem,
    own_code_sem,
    in_sem,
    plan_sem,
):
    n_group, n_blk, steps, cap, row_tiles, ctx_tiles, tile = sizes
    slots = n_group * cap
    group = lax.axis_index("group")
    blk = lax.axis_index("blk")
    right = lax.rem(blk + 1, n_blk)
    left = lax.rem(blk + n_blk - 1, n_blk)

    def peer(j):
        return lax.rem(group + j, n_group)

    def code_copy(j):
        return pltpu.make_async_remote_copy(
            src_ref=codes_ref.at[:, peer(j)],
            dst_ref=codebuf.at[j],
            send_sem=code_send.at[j],
            recv_sem=code_recv.at[j],
            device_id={"group": peer(j)},
            device_id_type=MESH,
        )

    def weight_copy(stop, j):
        return pltpu.make_async_remote_copy(
            src_ref=weights_hbm.at[peer(j), stop],
            dst_ref=wbuf.at[pl.ds(stop * slots + j * cap, cap)],
            send_sem=w_send.at[stop, j],
            recv_sem=w_recv.at[stop, j],
            device_id={"group": peer(j)},
            device_id_type=MESH,
        )

    def own_copy(stop):
        return pltpu.make_async_copy(
            weights_hbm.at[group, stop],
            wbuf.at[pl.ds(stop * slots, cap)],
            own_sem.at[stop],
        )

    def own_code():
        return pltpu.make_async_copy(codes_ref.at[:, group], codebuf.at[0], own_code_sem)

    def hop_copy(stop, c):
        return pltpu.make_async_remote_copy(
            src_ref=outgo.at[stop, c],
            dst_ref=held.at[stop, c],
            send_sem=hop_send.at[stop, c],
            recv_sem=hop_recv.at[stop, c],
            device_id={"blk": right},
            device_id_type=MESH,
        )

    def state_copy(stop, c):
        return pltpu.make_async_remote_copy(
            src_ref=out_state.at[stop, c],
            dst_ref=held_state.at[stop, c],
            send_sem=st_send.at[stop, c],
            recv_sem=st_recv.at[stop, c],
            device_id={"blk": right},
            device_id_type=MESH,
        )

    barrier = pltpu.get_barrier_semaphore()
    pl.semaphore_signal(barrier, inc=1, device_id={"blk": left}, device_id_type=MESH)
    for j in range(1, n_group):
        pl.semaphore_signal(
            barrier, inc=1, device_id={"group": peer(j)}, device_id_type=MESH
        )
    vertex_in = pltpu.make_async_copy(vertex_hbm, vout, in_sem.at[0])
    context_in = pltpu.make_async_copy(context_hbm, c32, in_sem.at[1])
    vstate_in = pltpu.make_async_copy(vstate_hbm, vsout, in_sem.at[2])
    cstate_in = pltpu.make_async_copy(cstate_hbm, held_state.at[0], in_sem.at[3])
    vstate_in.start()
    cstate_in.start()
    context_in.start()
    vertex_in.start()
    own_code().start()
    for stop in range(steps):
        own_copy(stop).start()
    pl.semaphore_wait(barrier, n_group)

    for j in range(1, n_group):
        code_copy(j).start()
    for stop in range(steps):
        for j in range(1, n_group):
            weight_copy(stop, j).start()

    vstate_in.wait()
    cstate_in.wait()
    context_in.wait()
    vertex_in.wait()
    for r in range(row_tiles):
        rows = slice(r * tile, (r + 1) * tile)
        vb[rows, :] = vout[rows, :].astype(jnp.bfloat16)
        vcol[rows, :] = jnp.broadcast_to(to_column(vsout[r : r + 1, :]), (tile, tile))
    for c in range(ctx_tiles):
        held[0, c] = c32[c].astype(jnp.bfloat16)

    own_code().wait()
    for j in range(1, n_group):
        code_copy(j).wait_recv()
    codes = [codebuf[j, k] for j in range(n_group) for k in range(cap)]
    lane = lax.broadcasted_iota(jnp.int32, codes[0].shape, 1)
    upto = jnp.zeros_like(lane)
    below = jnp.zeros_like(lane)
    order = jnp.zeros_like(lane)
    for n, code in enumerate(codes):
        upto = upto + jnp.where(code <= lane, 1, 0)
        below = below + jnp.where(code < lane, 1, 0)
        rank = jnp.zeros_like(lane)
        for m, other in enumerate(codes):
            if m < n:
                rank = rank + jnp.where(other <= code, 1, 0)
            elif m > n:
                rank = rank + jnp.where(other < code, 1, 0)
        order = order + jnp.where(rank == lane, n, 0)
    plan_vmem[0] = upto
    plan_vmem[1] = below
    plan_vmem[2] = order
    plan_copy = pltpu.make_async_copy(plan_vmem, plan, plan_sem)
    plan_copy.start()
    prefix[0] = jnp.zeros((tile, tile), jnp.float32)
    plan_copy.wait()

    width = vb.shape[1]
    batch = 1
    spread_mean = jnp.full((width, tile), 1.0 / width, jnp.bfloat16)

    def wide(value):
        return jnp.concatenate([value] * (width // tile), axis=1)

    def mean_square(grad):
        return jnp.dot(
            (grad * grad).astype(jnp.bfloat16), spread_mean, preferred_element_type=jnp.float32
        )

    def one_stop(s, first, last):
        own_copy(s).wait()
        for j in range(1, n_group):
            weight_copy(s, j).wait_recv()

        for n in range(slots):
            stage[n] = wbuf[s * slots + n]
        total = jnp.zeros((tile, tile), jnp.float32)
        for n in range(slots):
            total = total + 0.5 * stage[plan[2, s, n]].astype(jnp.float32)
            prefix[n + 1] = total

        def pair_gradients(first_tile):
            tiles = range(first_tile, first_tile + batch)
            if not first:
                for c in tiles:
                    hop_copy(s, c).wait_recv()
                    state_copy(s, c).wait_recv()
            ctx = held[s, first_tile : first_tile + batch].reshape(batch * tile, width)
            half_logits = lax.dot_general(
                vb[...],
                ctx * jnp.bfloat16(0.5),
                (((1,), (1,)), ((), ())),
                preferred_element_type=jnp.float32,
            )
            for r in range(row_tiles):
                rows = slice(r * tile, (r + 1) * tile)
                for i, c in enumerate(tiles):
                    pair = c * row_tiles + r
                    negative = jnp.float32(0.0)
                    for n in range(negs_ref.shape[1]):
                        negative = negative + jnp.where(
                            negs_ref[s, n, r] == c, 0.5 * NEG_WEIGHT, 0.0
                        )
                    weight = prefix[plan[0, s, pair]] - prefix[plan[1, s, pair]]
                    part = half_logits[rows, i * tile : (i + 1) * tile]
                    g = (negative + weight) * jnp.tanh(part) + (negative - weight)
                    gbuf[rows, c * tile : (c + 1) * tile] = g.astype(jnp.bfloat16)

        def context_update(first_tile):
            grads = lax.dot_general(
                gbuf[:, first_tile * tile : (first_tile + batch) * tile],
                vb[...],
                (((0,), (0,)), ((), ())),
                preferred_element_type=jnp.float32,
            )
            means = mean_square(grads)
            for i in range(batch):
                c = first_tile + i
                part = slice(i * tile, (i + 1) * tile)
                before = jnp.broadcast_to(to_column(held_state[s, c]), (tile, tile))
                state = before + means[part]
                old = c32[c] if first else held[s, c].astype(jnp.float32)
                new = old - grads[part] * wide(LEARNING * lax.rsqrt(state))
                state_row = to_row(state)
                if last:
                    cout[c] = new
                    csout[c] = state_row
                else:
                    outgo[s + 1, c] = new.astype(jnp.bfloat16)
                    out_state[s + 1, c] = state_row
                    hop_copy(s + 1, c).start()
                    state_copy(s + 1, c).start()

        for c in range(0, ctx_tiles, batch):
            pair_gradients(c)
            context_update(c)

        block = held[s].reshape(ctx_tiles * tile, width)
        half = row_tiles // 2
        for h in range(2):
            span = slice(h * half * tile, (h + 1) * half * tile)
            grads = jnp.dot(gbuf[span, :], block, preferred_element_type=jnp.float32)
            state = vcol[span, :] + mean_square(grads)
            new = vout[span, :] - grads * wide(LEARNING * lax.rsqrt(state))
            vcol[span, :] = state
            vout[span, :] = new
            vb[span, :] = new.astype(jnp.bfloat16)

    def middle_stop(s, _):
        one_stop(s, False, False)
        return 0

    one_stop(0, True, steps == 1)
    if steps > 2:
        lax.fori_loop(1, steps - 1, middle_stop, 0)
    if steps > 1:
        one_stop(steps - 1, False, True)

    for r in range(row_tiles):
        vsout[r : r + 1, :] = to_row(vcol[r * tile : (r + 1) * tile, :])

    for j in range(1, n_group):
        code_copy(j).wait_send()
    for stop in range(steps):
        for j in range(1, n_group):
            weight_copy(stop, j).wait_send()
    for stop in range(1, steps):
        for c in range(ctx_tiles):
            hop_copy(stop, c).wait_send()
            state_copy(stop, c).wait_send()


def put_out(*refs):
    count = len(refs) // 2
    sems = refs[-1]
    copies = [
        pltpu.make_async_copy(refs[i], refs[count + i], sems.at[i]) for i in range(count)
    ]
    for copy in copies:
        copy.start()
    for copy in copies:
        copy.wait()


def body(
    n_group,
    n_blk,
    vertex,
    vertex_state,
    context,
    context_state,
    tile_weights,
    tile_rows,
    tile_cols,
    tile_counts,
    negatives,
):
    steps, cap, tile = tile_weights.shape[3], tile_weights.shape[4], tile_weights.shape[5]
    width = vertex.shape[1]
    row_tiles, ctx_tiles = vertex.shape[0] // tile, context.shape[0] // tile
    pairs = row_tiles * ctx_tiles
    slots = n_group * cap
    assert pairs < tile and slots < tile

    def spread(ids):
        return jnp.broadcast_to(
            ids.transpose(2, 0, 1)[..., None], (cap, n_group, steps, tile)
        )

    used = (
        lax.broadcasted_iota(jnp.int32, (cap, n_group, steps, tile), 0)
        < tile_counts[0, 0][None, :, :, None]
    )
    codes = jnp.where(
        used, spread(tile_cols[0, 0]) * row_tiles + spread(tile_rows[0, 0]), pairs
    )
    sizes = (n_group, n_blk, steps, cap, row_tiles, ctx_tiles, tile)
    vmem = pl.BlockSpec(memory_space=pltpu.VMEM)
    hbm = pl.BlockSpec(memory_space=pltpu.HBM)
    f32, bf16 = jnp.float32, jnp.bfloat16
    dma = pltpu.SemaphoreType.DMA
    outs = (
        jax.ShapeDtypeStruct((row_tiles * tile, width), f32),
        jax.ShapeDtypeStruct((row_tiles, tile), f32),
        jax.ShapeDtypeStruct((ctx_tiles, tile, width), f32),
        jax.ShapeDtypeStruct((ctx_tiles, 1, tile), f32),
    )
    results = pl.pallas_call(
        functools.partial(kernel, sizes),
        out_shape=outs,
        in_specs=[vmem, pl.BlockSpec(memory_space=pltpu.SMEM)] + [hbm] * 5,
        out_specs=(vmem,) * 4,
        scratch_shapes=[
            pltpu.VMEM((row_tiles * tile, width), bf16),
            pltpu.VMEM((row_tiles * tile, tile), f32),
            pltpu.VMEM((steps, ctx_tiles, tile, width), bf16),
            pltpu.VMEM((steps, ctx_tiles, tile, width), bf16),
            pltpu.VMEM((steps, ctx_tiles, 1, tile), f32),
            pltpu.VMEM((steps, ctx_tiles, 1, tile), f32),
            pltpu.VMEM((ctx_tiles, tile, width), f32),
            pltpu.VMEM((row_tiles * tile, ctx_tiles * tile), bf16),
            pltpu.VMEM((slots + 1, tile, tile), f32),
            pltpu.VMEM((slots, tile, tile), bf16),
            pltpu.VMEM((steps * slots, tile, tile), bf16),
            pltpu.VMEM((n_group, cap, steps, tile), jnp.int32),
            pltpu.VMEM((3, steps, tile), jnp.int32),
            pltpu.SMEM((3, steps, tile), jnp.int32),
            dma((steps, ctx_tiles)),
            dma((steps, ctx_tiles)),
            dma((steps, ctx_tiles)),
            dma((steps, ctx_tiles)),
            dma((steps, n_group)),
            dma((steps, n_group)),
            dma((n_group,)),
            dma((n_group,)),
            dma((steps,)),
            dma,
            dma((4,)),
            dma,
        ],
        compiler_params=pltpu.CompilerParams(
            collective_id=0, has_side_effects=True, vmem_limit_bytes=VMEM_LIMIT
        ),
    )(
        codes,
        negatives[0, 0].transpose(0, 2, 1),
        vertex,
        vertex_state.reshape(row_tiles, tile),
        context.reshape(ctx_tiles, tile, width),
        context_state.reshape(ctx_tiles, 1, tile),
        tile_weights.reshape(n_group, steps, cap, tile, tile),
    )
    vout, vsout, cout, csout = pl.pallas_call(
        put_out,
        out_shape=outs,
        in_specs=[vmem] * 4,
        out_specs=(hbm,) * 4,
        scratch_shapes=[dma((4,))],
        compiler_params=pltpu.CompilerParams(vmem_limit_bytes=1024 * 1024),
    )(*results)
    return (
        vout,
        vsout.reshape(-1),
        cout.reshape(ctx_tiles * tile, width),
        csout.reshape(-1),
    )


def solution(mesh):
    in_specs = (
        P(("group", "blk"), None),
        P(("group", "blk")),
        P(("group", "blk"), None),
        P(("group", "blk")),
        P("group", "blk", None, None, None, None, None),
        P("group", "blk", None, None, None),
        P("group", "blk", None, None, None),
        P("group", "blk", None, None),
        P("group", "blk", None, None, None),
    )
    out_specs = (
        P(("group", "blk"), None),
        P(("group", "blk")),
        P(("group", "blk"), None),
        P(("group", "blk")),
    )
    step = functools.partial(body, mesh.shape["group"], mesh.shape["blk"])
    return jax.shard_map(step, mesh=mesh, in_specs=in_specs, out_specs=out_specs, check_vma=False)
```
